256 devices in a mesh: section: 8 (over z_lo, x), dp: 32 (over z_hi, y, core).
Axes of the slice: x: 4, y: 4, z: 8 (z_hi: 4, z_lo: 2; z = z_hi * 2 + z_lo), core: 2. Of those that a mesh axis runs over, the one named last changes fastest.
Arguments:
- incoming: bfloat16 [8, 4, 4096, 256], P('section', None, 'dp'), may hold values from -6 to 6
- feed: bfloat16 [4, 4, 4096, 256], P(None, None, 'dp'), may hold values from -6 to 6
- plan: int32 [1, 32], P(None, 'dp'), may hold values from 0 to 3, as said below
- weights: bfloat16 [8, 2, 27, 256, 256], P('section'), may hold values from -0.078125 to 0.078125
- momentum: float32 [8, 2, 27, 256, 256], P('section', None, None, 'dp'), may hold values from -6 to 6
Outputs:
- upstream: bfloat16 [2, 8, 4, 4096, 256], P(None, 'section', None, 'dp')
- new_momentum: float32 [8, 2, 27, 256, 256], P('section', None, None, 'dp')
The draws below stay inside these ranges and needn't reach their ends.
Inputs may be any that keep to these rules, and one draw needn't show every extreme that they name: `plan`: every micro-batch of the pool is taken by some tile in some tick.
All inputs are finite; a program needn't handle non-finite values.
Results may differ from the reference program's by a relative error of at most 0.014.
Values may be sent and summed in bfloat16 or wider, within the bound.
No kernel may reach another device: no remote copies, remote signals or barrier semaphores. Data moves between devices by JAX's collectives and lax.ppermute only.
A program may use at most 128 MiB of HBM per device.

```python
import jax
import jax.numpy as jnp
from jax import lax

C = 256
TD = 2
TH = 8
TW = 8
TICKS = 2
POOL = 4
VOX = 128
VOX_ALL = 4096
N_SECTION = 8
N_DP = 32


def draw_plan(key, part):
    count = (TICKS - 1) * N_DP
    order = jax.random.permutation(key, count)
    return (order % POOL).reshape(TICKS - 1, N_DP).astype(jnp.int32)


def with_spikes(values, rng, source, target, blocks, factor):
    def block_of(position):
        return (jnp.arange(values.shape[position]) // (values.shape[position] // blocks)).reshape((-1,) + (1,) * (values.ndim - 1 - position))

    first = jax.random.permutation(rng, blocks)[block_of(target)]
    second = (block_of(target) + blocks // 2) % blocks
    return jnp.where((block_of(source) == first) | (block_of(source) == second), factor * values, values)


def block_scale(stream_key, shape, cuts, low, top_value):
    gain, own = 1.0, jax.random.fold_in(stream_key, 6)
    for position, parts in cuts:
        steps = jnp.exp(jax.random.uniform(jax.random.fold_in(own, position), (parts,), jnp.float32, low / len(cuts), top_value / len(cuts)))
        gain = gain * jnp.repeat(steps, shape[position] // parts).reshape([-1 if axis == position else 1 for axis in range(len(shape))])
    return gain


def normal_values(own_key, shape, deviation, reach, cuts=(), dtype=jnp.bfloat16):
    drawn = jax.random.normal(own_key, shape, jnp.float32) * deviation
    if len(cuts) > 0:
        drawn = block_scale(own_key, shape, cuts, -0.22, 0.18) * drawn
    return jnp.clip(drawn, min=-reach, max=reach).astype(dtype)


def noise_with(rng, extent, scale, reach, cuts, heavy, kind=jnp.bfloat16):
    drawn = scale * jax.random.normal(rng, extent, jnp.float32)
    if cuts:
        drawn = drawn * block_scale(rng, extent, cuts, -0.22, 0.18)
    return jnp.clip(with_spikes(drawn, jax.random.fold_in(rng, 3), *heavy), -reach, reach).astype(kind)


def setup_inputs(seed: int = 0) -> dict:
    seeds = jax.random.split(jax.random.key(seed), 6)
    incoming = noise_with(seeds[0], (N_SECTION, 4, VOX_ALL, C), 1.0, 6.0, ((0, 8), (2, 32)), (2, 3, 32, 2.75))
    feed = normal_values(seeds[1], (POOL, 4, VOX_ALL, C), 1.0, 6.0, ((2, 32),))
    plan = draw_plan(jax.random.fold_in(seeds[5], 71), 0)
    weights = normal_values(seeds[3], (N_SECTION, 2, 27, C, C), (27 * C) ** -0.5, 0.078125, ((0, 8),))
    momentum = normal_values(seeds[4], (N_SECTION, 2, 27, C, C), 1.0, 6.0, ((0, 8), (3, 32)), jnp.float32)
    return {"incoming": incoming, "feed": feed, "plan": plan, "weights": weights, "momentum": momentum}


def make_patches(act, sign):
    volume = act.reshape(TD, TH, TW, act.shape[-1])
    padded = jnp.pad(volume, ((1, 1), (1, 1), (1, 1), (0, 0)))
    pieces = []
    for depth in (-1, 0, 1):
        for height in (-1, 0, 1):
            for width in (-1, 0, 1):
                start_d = 1 + sign * depth
                start_h = 1 + sign * height
                start_w = 1 + sign * width
                cut = padded[start_d:start_d + TD, start_h:start_h + TH, start_w:start_w + TW]
                pieces.append(cut.reshape(VOX, act.shape[-1]))
    return jnp.stack(pieces, axis=1)

def silu_grad(value):
    sig = jax.nn.sigmoid(value)
    return sig * (1.0 + value * (1.0 - sig))

def tile_back(inputs, weight):
    y_one = inputs[0]
    y_two = inputs[1]
    dy_one = inputs[2].astype(jnp.float32)
    dy_two = inputs[3]
    weight_f = weight[0].astype(jnp.float32)
    weight_g = weight[1].astype(jnp.float32)
    y_one_f = y_one.astype(jnp.float32)
    act_one = jax.nn.silu(y_one_f).astype(jnp.bfloat16)
    patch_one = make_patches(act_one, 1).astype(jnp.float32)
    g_out = jnp.einsum('vtc,toc->vo', patch_one, weight_g)
    x_two = (y_two.astype(jnp.float32) - g_out).astype(jnp.bfloat16)
    grad_g = jnp.einsum('vo,vti->toi', dy_two.astype(jnp.float32), patch_one)
    back_two = make_patches(dy_two, -1).astype(jnp.float32)
    d_act_one = jnp.einsum('vto,toi->vi', back_two, weight_g)
    dx_one = (dy_one + d_act_one * silu_grad(y_one_f)).astype(jnp.bfloat16)
    x_two_f = x_two.astype(jnp.float32)
    act_two = jax.nn.silu(x_two_f).astype(jnp.bfloat16)
    patch_two = make_patches(act_two, 1).astype(jnp.float32)
    f_out = jnp.einsum('vtc,toc->vo', patch_two, weight_f)
    x_one = (y_one_f - f_out).astype(jnp.bfloat16)
    grad_f = jnp.einsum('vo,vti->toi', dx_one.astype(jnp.float32), patch_two)
    back_one = make_patches(dx_one, -1).astype(jnp.float32)
    d_act_two = jnp.einsum('vto,toi->vi', back_one, weight_f)
    dx_two = (dy_two.astype(jnp.float32) + d_act_two * silu_grad(x_two_f)).astype(jnp.bfloat16)
    return (jnp.stack([x_one, x_two, dx_one, dx_two]), jnp.stack([grad_f, grad_g]))

def section_outs(pair):
    inputs, weight = pair
    tiles = inputs.reshape(4, N_DP, VOX, C)

    def one_tile(carry, index):
        outs, grads = tile_back(tiles[:, index], weight)
        return (carry, outs)
    unused, outs = lax.scan(one_tile, jnp.zeros((), jnp.float32), jnp.arange(N_DP))
    return jnp.transpose(outs, (1, 0, 2, 3)).reshape(4, VOX_ALL, C)

def section_grads(pair):
    seen, weight = pair
    tiles = seen.reshape(TICKS, 4, N_DP, VOX, C)

    def one_tile(carry, index):
        term = jnp.zeros((2, 27, C, C), jnp.float32)
        for tick in range(TICKS):
            outs, grads = tile_back(tiles[tick, :, index], weight)
            term = term + grads
        part = term.astype(jnp.bfloat16).astype(jnp.float32)
        return (carry + part, None)
    zero = jnp.zeros((2, 27, C, C), jnp.float32)
    total, unused = lax.scan(one_tile, zero, jnp.arange(N_DP))
    return total

def reference(incoming, feed, plan, weights, momentum):
    current = incoming
    results = []
    seen = []
    for tick in range(TICKS):
        seen.append(current)
        outs = lax.map(section_outs, (current, weights))
        results.append(outs)
        if tick + 1 < TICKS:
            pool = feed.reshape(POOL, 4, N_DP, VOX, C)
            picks = plan[tick]
            chosen = pool[picks, :, jnp.arange(N_DP)]
            chosen = jnp.transpose(chosen, (1, 0, 2, 3)).reshape(4, VOX_ALL, C)
            current = jnp.concatenate([outs[1:], chosen[None]], axis=0)
    seen_all = jnp.stack(seen, axis=1)
    grad_total = lax.map(section_grads, (seen_all, weights))
    upstream = jnp.stack(results)
    new_momentum = 0.9 * momentum + grad_total / (N_DP * TICKS)
    return (upstream, new_momentum)
```

```python
import functools

import jax
import jax.numpy as jnp
from jax import lax
from jax.experimental import pallas as pl
from jax.experimental.pallas import tpu as pltpu
from jax.sharding import PartitionSpec as P

TD, TH, TW = 2, 8, 8
VOX = TD * TH * TW
CH = 256
HALF = 128
LINE = TD * TW
TICKS = 2
NZ, NY, NC = 4, 4, 2
QUARTER = 64
F32, BF16 = jnp.float32, jnp.bfloat16
F, G = 0, 1
FIRST = {F: 1, G: 3}
SECOND = {F: 3, G: 1}
KEEP = {b: (0, SECOND[b]) for b in (F, G)}
SEND = {b: (FIRST[b], FIRST[b] ^ SECOND[b]) for b in (F, G)}
VMEM = pl.BlockSpec(memory_space=pltpu.VMEM)


def rank_of(z, y, c):
    return ((z % NZ) * NY + y % NY) * NC + c % NC


def dp_permute(array, move):
    pairs = []
    for z in range(NZ):
        for y in range(NY):
            for c in range(NC):
                pairs.append((rank_of(z, y, c), rank_of(*move(z, y, c))))
    return lax.ppermute(array, "dp", pairs)


def from_next_section(array):
    size = lax.axis_size("section")
    return lax.ppermute(array, "section", [(i, i - 1) for i in range(1, size)])


def to_hdw(x):
    return jnp.concatenate([x[64 * d + 8 * h : 64 * d + 8 * h + 8] for h in range(TH) for d in range(TD)], axis=0)


def to_dhw(x):
    return jnp.concatenate([x[16 * h + 8 * d : 16 * h + 8 * d + 8] for d in range(TD) for h in range(TH)], axis=0)


def silu_pair(u):
    sig = jax.nn.sigmoid(u)
    return u * sig, sig * (1.0 + u * (1.0 - sig))


def moved(x, dd, dw):
    row = lax.broadcasted_iota(jnp.int32, x.shape, 0)
    ok = None
    if dw:
        x = pltpu.roll(x, (-dw) % VOX, 0)
        w = row % TW + dw
        ok = (w >= 0) & (w < TW)
    if dd:
        pieces = [x[LINE * h + 8 * (1 - d) : LINE * h + 8 * (1 - d) + 8] for h in range(TH) for d in range(TD)]
        x = jnp.concatenate(pieces, axis=0)
        d = (row // TW) % TD + dd
        inside = (d >= 0) & (d < TD)
        ok = inside if ok is None else ok & inside
    if ok is not None:
        x = jnp.where(ok, x, 0.0)
    return x.astype(BF16)


def fill(buf, x, dd, sign):
    zero = jnp.zeros((LINE, CH), BF16)
    for dw in (-1, 0, 1):
        m = moved(x, sign * dd, sign * dw)
        for dh in (-1, 0, 1):
            k = 3 * (dh + 1) + dw + 1
            cols = slice(CH * k, CH * k + CH)
            if sign * dh == 0:
                buf[:, cols] = m
            elif sign * dh == 1:
                buf[: VOX - LINE, cols] = m[LINE:]
                buf[VOX - LINE :, cols] = zero
            else:
                buf[LINE:, cols] = m[: VOX - LINE]
                buf[:LINE, cols] = zero


def convolve(step, act, err, w_ref, buf_a, buf_e, acc_a, acc_e):
    for i, dd in enumerate((-1, 0, 1)):

        @pl.when(step == i)
        def _():
            fill(buf_a, act, dd, 1)
            fill(buf_e, err, dd, -1)

    ahead = None
    for k in range(9):
        term = lax.dot_general(
            buf_a[:, CH * k : CH * k + CH], w_ref[k], (((1,), (1,)), ((), ())), preferred_element_type=F32
        )
        ahead = term if ahead is None else ahead + term
    back = jnp.dot(buf_e[...], w_ref[...].reshape(9 * CH, CH), preferred_element_type=F32)

    @pl.when(step == 0)
    def _():
        acc_a[...] = ahead
        acc_e[...] = back

    @pl.when(step > 0)
    def _():
        acc_a[...] += ahead
        acc_e[...] += back


def pick(place, below, chosen):
    return jnp.where(place[3] == 1, chosen, below)


def half_g_kernel(place, *refs, picks):
    if picks:
        late, early, chosen, w_ref, out, give, mine, *scratch = refs
        y_one, dy_two, y_two, dy_one = (
            pick(place, late[0].astype(F32), chosen[0, 0].astype(F32)),
            pick(place, late[1].astype(F32), chosen[0, 3].astype(F32)),
            pick(place, early[0].astype(F32), chosen[0, 1].astype(F32)),
            pick(place, early[1].astype(F32), chosen[0, 2].astype(F32)),
        )
    else:
        incoming, w_ref, out, give, mine, *scratch = refs
        y_one, y_two, dy_one, dy_two = [incoming[i].astype(F32) for i in range(4)]
    step = pl.program_id(0)
    u = to_hdw(y_one)
    act, slope = silu_pair(u)
    act = act.astype(BF16).astype(F32)
    err = to_hdw(dy_two)
    convolve(step, act, err, w_ref, *scratch)
    acc_a, acc_e = scratch[2:]

    @pl.when(step == 2)
    def _():
        x_two = (to_hdw(y_two) - acc_a[...]).astype(BF16).astype(F32)
        dx_one = (to_hdw(dy_one) + acc_e[...] * slope).astype(BF16).astype(F32)
        out[0] = to_dhw(x_two).astype(BF16)
        out[1] = to_dhw(dx_one).astype(BF16)
        act_two = silu_pair(x_two)[0]
        core, y, z = place[0], place[1], place[2]
        for b, a, e in ((F, act_two, dx_one), (G, act, err)):
            low, high = a[:, :HALF], a[:, HALF:]
            mine[b] = jnp.where(core == 0, low, high).astype(BF16)
            give[b, :VOX] = jnp.where(core == 0, high, low).astype(BF16)
            flipped = e.T.astype(BF16)
            for zz in range(NZ):
                for yy in range(NY):
                    row = VOX + QUARTER * ((yy - y) & 3) + 16 * (zz ^ z)
                    start = QUARTER * zz + 16 * yy
                    give[b, pl.ds(pl.multiple_of(row, 16), 16)] = flipped[start : start + 16]


def half_f_kernel(place, *refs, picks):
    if picks:
        late, early, mid, chosen, first_early, first_late, w_ref, out, *scratch = refs
        y_one = pick(place, late[0].astype(F32), chosen[0, 0].astype(F32))
        dy_two = pick(place, late[1].astype(F32), chosen[0, 3].astype(F32))
    else:
        incoming, mid, w_ref, out, *scratch = refs
        y_one, dy_two = incoming[0].astype(F32), incoming[3].astype(F32)
    step = pl.program_id(0)
    x_two, dx_one = mid[0].astype(F32), mid[1].astype(F32)
    act, slope = silu_pair(to_hdw(x_two))
    act = act.astype(BF16).astype(F32)
    convolve(step, act, to_hdw(dx_one), w_ref, *scratch)
    acc_a, acc_e = scratch[2:]

    @pl.when(step == 2)
    def _():
        x_one = (y_one - to_dhw(acc_a[...])).astype(BF16)
        dx_two = (dy_two + to_dhw(acc_e[...] * slope)).astype(BF16)
        if picks:
            out[0, 0] = first_late[0]
            out[0, 1] = first_early[0]
            out[0, 2] = first_early[1]
            out[0, 3] = first_late[1]
            out[1, 0] = x_one
            out[1, 1] = mid[0]
            out[1, 2] = mid[1]
            out[1, 3] = dx_two
        else:
            out[0] = x_one
            out[1] = dx_two


def whole(shape):
    return pl.BlockSpec(shape, lambda i, place: (0,) * len(shape))


def call_half(kernel, place, args, weights, branch, out_shapes, picks, name):
    specs = []
    for a in args:
        if a.ndim == 4:
            specs.append(pl.BlockSpec((1,) + a.shape[1:], lambda i, place: (place[4], 0, 0, 0)))
        else:
            specs.append(whole(a.shape))
    specs.append(pl.BlockSpec((None, 9, CH, CH), lambda i, place: (branch, i, 0, 0)))
    single = len(out_shapes) == 1
    shapes = [jax.ShapeDtypeStruct(s, BF16) for s in out_shapes]
    result = pl.pallas_call(
        functools.partial(kernel, picks=picks),
        grid_spec=pltpu.PrefetchScalarGridSpec(
            num_scalar_prefetch=1,
            grid=(3,),
            in_specs=specs,
            out_specs=[whole(s) for s in out_shapes],
            scratch_shapes=[pltpu.VMEM((VOX, 9 * CH), BF16)] * 2 + [pltpu.VMEM((VOX, CH), F32)] * 2,
        ),
        out_shape=shapes,
        compiler_params=pltpu.CompilerParams(vmem_limit_bytes=20 << 20),
        cost_estimate=pl.CostEstimate(flops=4 * 27 * VOX * CH * CH, bytes_accessed=27 * CH * CH * 2, transcendentals=0),
        name=name,
    )(place, *args, weights)
    return result[0] if single else result


def pack_kernel(mine, give, got, *outs):
    for by, out in zip((1, 2, 3), outs):
        rows = slice(VOX + QUARTER * by, VOX + QUARTER * by + QUARTER)
        out[:, 0, :VOX] = mine[...]
        out[:, 0, VOX:] = give[:, rows]
        out[:, 1, :VOX] = got[:, :VOX]
        out[:, 1, VOX:] = got[:, rows]


def gather_factors(give, mine):
    got = dp_permute(give, lambda z, y, c: (z, y, c + 1))
    shape = jax.ShapeDtypeStruct((2, 2, VOX + QUARTER, HALF), BF16)
    packed = pl.pallas_call(
        pack_kernel,
        out_shape=[shape] * 3,
        in_specs=[VMEM] * 3,
        out_specs=[VMEM] * 3,
        compiler_params=pltpu.CompilerParams(vmem_limit_bytes=8 << 20),
        cost_estimate=pl.CostEstimate(flops=0, bytes_accessed=1 << 20, transcendentals=0),
        name="pack",
    )(mine, give, got)
    parts = [dp_permute(p, lambda z, y, c, by=by: (z, y + by, c)) for by, p in zip((1, 2, 3), packed)]
    return (mine, give, got, *parts)


def products(refs, branch, lhs, rhs):
    mine, give, got, *parts = refs
    tiles = [(mine[branch], give[branch, VOX : VOX + QUARTER]), (got[branch, :VOX], got[branch, VOX : VOX + QUARTER])]
    for p in parts:
        for tile in range(2):
            tiles.append((p[branch, tile, :VOX], p[branch, tile, VOX:]))
    lane = lax.broadcasted_iota(jnp.int32, (QUARTER, VOX), 1)
    depth, width = (lane // TW) % TD, lane % TW
    zero = jnp.zeros((LINE, HALF), BF16)
    for index, (act, err) in enumerate(tiles):
        at = VOX * index
        rhs[0, at : at + LINE] = zero
        rhs[0, at + LINE : at + VOX] = act[: VOX - LINE]
        rhs[1, at : at + VOX] = act
        rhs[2, at : at + VOX - LINE] = act[LINE:]
        rhs[2, at + VOX - LINE : at + VOX] = zero
        err = err.astype(F32)
        for dd in (-1, 0, 1):
            for dw in (-1, 0, 1):
                x = err
                if dd or dw:
                    x = pltpu.roll(err, (TW * dd + dw) % VOX, 1)
                    ok = (depth - dd >= 0) & (depth - dd < TD) & (width - dw >= 0) & (width - dw < TW)
                    x = jnp.where(ok, x, 0.0)
                v = 3 * (dd + 1) + dw + 1
                lhs[QUARTER * v : QUARTER * v + QUARTER, at : at + VOX] = x.astype(BF16)
    return [jnp.dot(lhs[...], rhs[dh], preferred_element_type=F32) for dh in range(3)]


def first_grads_kernel(*refs):
    *ins, out, lhs, rhs = refs
    for branch in (F, G):
        for dh, value in enumerate(products(ins, branch, lhs, rhs)):
            out[branch, dh] = value


def last_grads_kernel(*refs, branch):
    *ins, before, keep, send, lhs, rhs = refs
    for dh, value in enumerate(products(ins, branch, lhs, rhs)):
        value = (value + before[branch, dh]).astype(BF16)
        for dd in range(3):
            for dw in range(3):
                for slots, out in ((KEEP[branch], keep), (SEND[branch], send)):
                    for i, slot in enumerate(slots):
                        row = QUARTER * (3 * dd + dw) + 16 * slot
                        out[i, 9 * dd + 3 * dh + dw] = value[row : row + 16]


def grad_call(kernel, ins, out_shape, flops, name):
    return pl.pallas_call(
        kernel,
        out_shape=out_shape,
        in_specs=[VMEM] * len(ins),
        out_specs=jax.tree.map(lambda s: VMEM, out_shape),
        scratch_shapes=[pltpu.VMEM((9 * QUARTER, 8 * VOX), BF16), pltpu.VMEM((3, 8 * VOX, HALF), BF16)],
        compiler_params=pltpu.CompilerParams(vmem_limit_bytes=24 << 20),
        cost_estimate=pl.CostEstimate(flops=flops, bytes_accessed=4 << 20, transcendentals=0),
        name=name,
    )(*ins)


def middle_kernel(place, keep, got, mine, cross, same, chip):
    core = place[0]
    own = keep[0].astype(F32) + got[0].astype(F32)
    other = keep[1].astype(F32) + got[1].astype(F32)
    low, high = own[:, :8], own[:, 8:]
    mine[...] = jnp.where(core == 0, low, high)
    chip[...] = jnp.where(core == 0, high, low).astype(BF16)
    low, high = other[:, :8], other[:, 8:]
    same[...] = jnp.where(core == 0, low, high).astype(BF16)
    cross[...] = jnp.where(core == 0, high, low).astype(BF16)


def reduce_z(place, keep, send, branch):
    got = dp_permute(send, lambda z, y, c: (z ^ FIRST[branch], y, c))
    piece = (27, 8, HALF)
    mine, cross, same, chip = pl.pallas_call(
        middle_kernel,
        out_shape=[jax.ShapeDtypeStruct(piece, F32)] + [jax.ShapeDtypeStruct(piece, BF16)] * 3,
        in_specs=[pl.BlockSpec(memory_space=pltpu.SMEM), VMEM, VMEM],
        out_specs=[VMEM] * 4,
        compiler_params=pltpu.CompilerParams(vmem_limit_bytes=8 << 20),
        cost_estimate=pl.CostEstimate(flops=0, bytes_accessed=1 << 20, transcendentals=0),
        name=f"middle_{branch}",
    )(place, keep, got)
    same = dp_permute(same, lambda z, y, c: (z ^ SECOND[branch], y, c))
    cross = dp_permute(cross, lambda z, y, c: (z ^ SECOND[branch], y, c + 1))
    chip = dp_permute(chip, lambda z, y, c: (z, y, c + 1))
    return mine, same, cross, chip


def update_kernel(place, *refs, scale):
    *terms, momentum, out = refs
    core = place[0]
    for branch in (F, G):
        mine, same, cross, chip = terms[4 * branch : 4 * branch + 4]
        own = mine[...] + same[...].astype(F32)
        other = cross[...].astype(F32) + chip[...].astype(F32)
        low = jnp.where(core == 0, own, other)
        high = jnp.where(core == 0, other, own)
        out[branch, :, :, :HALF] = 0.9 * momentum[branch, :, :, :HALF] + low * scale
        out[branch, :, :, HALF:] = 0.9 * momentum[branch, :, :, HALF:] + high * scale


def body(incoming, feed, plan, weights, momentum):
    replicas = lax.axis_size("dp")
    rank = lax.axis_index("dp")
    z, y, c = rank // (NY * NC), (rank // NC) % NY, rank % NC
    is_last = (lax.axis_index("section") == lax.axis_size("section") - 1).astype(jnp.int32)
    slot = jnp.arange(8, dtype=jnp.int32)
    place = jnp.zeros((8,), jnp.int32)
    for i, value in enumerate((c, y, z, is_last, plan[0, 0])):
        place = jnp.where(slot == i, value, place)
    weights = weights[0]
    incoming = incoming[0]
    pair = (2, VOX, CH)
    mid_shapes = [pair, (2, VOX + CH, HALF), (2, VOX, HALF)]
    early, give, mine = call_half(half_g_kernel, place, [incoming], weights, G, mid_shapes, False, "half_g0")
    factors0 = gather_factors(give, mine)
    late = call_half(half_f_kernel, place, [incoming, early], weights, F, [pair], False, "half_f0")
    y_early, y_late = from_next_section(early), from_next_section(late)
    flops = 4 * 27 * QUARTER * HALF * 8 * VOX
    before = grad_call(
        first_grads_kernel, factors0, jax.ShapeDtypeStruct((2, 3, 9 * QUARTER, HALF), F32), flops, "grads0"
    )
    mid, give, mine = call_half(
        half_g_kernel, place, [y_late, y_early, feed], weights, G, mid_shapes, True, "half_g1"
    )
    factors1 = gather_factors(give, mine)
    upstream = call_half(
        half_f_kernel,
        place,
        [y_late, y_early, mid, feed, early, late],
        weights,
        F,
        [(2, 4, VOX, CH)],
        True,
        "half_f1",
    )
    terms = {}
    block = jax.ShapeDtypeStruct((2, 27, 16, HALF), BF16)
    for branch in (G, F):
        keep, send = grad_call(
            functools.partial(last_grads_kernel, branch=branch),
            (*factors1, before),
            [block, block],
            flops // 2,
            f"grads1_{branch}",
        )
        terms[branch] = reduce_z(place, keep, send, branch)
    new = pl.pallas_call(
        functools.partial(update_kernel, scale=1.0 / (replicas * TICKS)),
        out_shape=jax.ShapeDtypeStruct(momentum.shape[1:], F32),
        in_specs=[pl.BlockSpec(memory_space=pltpu.SMEM)] + [VMEM] * 9,
        out_specs=VMEM,
        compiler_params=pltpu.CompilerParams(vmem_limit_bytes=8 << 20),
        name="update",
    )(place, *terms[F], *terms[G], momentum[0])
    return (upstream[:, None], new[None])


def solution(mesh):
    in_specs = (
        P("section", None, "dp", None),
        P(None, None, "dp", None),
        P(None, "dp"),
        P("section", None, None, None, None),
        P("section", None, None, "dp", None),
    )
    out_specs = (P(None, "section", None, "dp", None), P("section", None, None, "dp", None))
    return jax.shard_map(body, mesh=mesh, in_specs=in_specs, out_specs=out_specs, check_vma=False)
```

```python
import functools

import jax
import jax.numpy as jnp
from jax import lax
from jax.experimental import pallas as pl
from jax.experimental.pallas import tpu as pltpu
from jax.sharding import PartitionSpec as P


TD, TH, TW = 2, 8, 8
VOX = TD * TH * TW
CH = 256
HALF = 128
LINE = TD * TW
TICKS = 2
NZ, NY, NC = 4, 4, 2
QUARTER = 64
F32, BF16 = jnp.float32, jnp.bfloat16
F, G = 0, 1
FIRST = {F: 1, G: 3}
SECOND = {F: 3, G: 1}
KEEP = {b: (0, SECOND[b]) for b in (F, G)}
SEND = {b: (FIRST[b], FIRST[b] ^ SECOND[b]) for b in (F, G)}
CHUNKS = 3
VMEM = pl.BlockSpec(memory_space=pltpu.VMEM)
SMEM = pl.BlockSpec(memory_space=pltpu.SMEM)
HBM = pl.BlockSpec(memory_space=pltpu.HBM)


def rank_of(z, y, c):
    return ((z % NZ) * NY + y % NY) * NC + c % NC


def dp_permute(array, move):
    pairs = []
    for z in range(NZ):
        for y in range(NY):
            for c in range(NC):
                pairs.append((rank_of(z, y, c), rank_of(*move(z, y, c))))
    return lax.ppermute(array, "dp", pairs)


def from_next_section(array):
    size = lax.axis_size("section")
    return lax.ppermute(array, "section", [(i, i - 1) for i in range(1, size)])


def to_hdw(x):
    return jnp.concatenate([x[64 * d + 8 * h : 64 * d + 8 * h + 8] for h in range(TH) for d in range(TD)], axis=0)


def to_dhw(x):
    return jnp.concatenate([x[16 * h + 8 * d : 16 * h + 8 * d + 8] for d in range(TD) for h in range(TH)], axis=0)


def silu_pair(u):
    sig = jax.nn.sigmoid(u)
    return u * sig, sig * (1.0 + u * (1.0 - sig))


def moved(x, dd, dw):
    row = lax.broadcasted_iota(jnp.int32, x.shape, 0)
    ok = None
    if dw:
        x = pltpu.roll(x, (-dw) % VOX, 0)
        w = row % TW + dw
        ok = (w >= 0) & (w < TW)
    if dd:
        pieces = [x[LINE * h + 8 * (1 - d) : LINE * h + 8 * (1 - d) + 8] for h in range(TH) for d in range(TD)]
        x = jnp.concatenate(pieces, axis=0)
        d = (row // TW) % TD + dd
        inside = (d >= 0) & (d < TD)
        ok = inside if ok is None else ok & inside
    if ok is not None:
        x = jnp.where(ok, x, 0.0)
    return x.astype(BF16)


def fill(buf, x, sign):
    zero = jnp.zeros((LINE, CH), BF16)
    for dd in (-1, 0, 1):
        for dw in (-1, 0, 1):
            m = moved(x, sign * dd, sign * dw)
            for dh in (-1, 0, 1):
                t = 9 * (dd + 1) + 3 * (dh + 1) + dw + 1
                cols = slice(CH * t, CH * t + CH)
                if sign * dh == 0:
                    buf[:, cols] = m
                elif sign * dh == 1:
                    buf[: VOX - LINE, cols] = m[LINE:]
                    buf[VOX - LINE :, cols] = zero
                else:
                    buf[LINE:, cols] = m[: VOX - LINE]
                    buf[:LINE, cols] = zero


def convolve(act, err, wait, w_ref, buf_a, buf_e):
    fill(buf_a, act, 1)
    fill(buf_e, err, -1)
    wait()
    back = jnp.dot(buf_e[...], w_ref[...].reshape(27 * CH, CH), preferred_element_type=F32)
    ahead = None
    for t in range(27):
        term = lax.dot_general(
            buf_a[:, CH * t : CH * t + CH], w_ref[t], (((1,), (1,)), ((), ())), preferred_element_type=F32
        )
        ahead = term if ahead is None else ahead + term
    return ahead, back


def pick(place, below, chosen):
    return jnp.where(place[3] == 1, chosen, below)


def fetches(w_hbm, w_vmem, branch, sems):
    size = 27 // CHUNKS
    copies = []
    for k in range(CHUNKS):
        taps = pl.ds(size * k, size)
        copies.append(pltpu.make_async_copy(w_hbm.at[branch, taps], w_vmem.at[taps], sems.at[CHUNKS * branch + k]))
    return copies


def half_g_kernel(place, *refs, picks):
    if picks:
        late, early, feed, w_g, out, give, mine, *bufs = refs
        chosen = feed.at[place[4]]
        y_one, dy_two, y_two, dy_one = (
            pick(place, late[0].astype(F32), chosen[0].astype(F32)),
            pick(place, late[1].astype(F32), chosen[3].astype(F32)),
            pick(place, early[0].astype(F32), chosen[1].astype(F32)),
            pick(place, early[1].astype(F32), chosen[2].astype(F32)),
        )

        def wait():
            pass

    else:
        incoming, w_hbm, out, give, mine, held, w_g, w_f, *bufs, sems = refs
        first = pltpu.make_async_copy(incoming, held, sems.at[2 * CHUNKS])
        first.start()
        copies_g, copies_f = fetches(w_hbm, w_g, G, sems), fetches(w_hbm, w_f, F, sems)
        for copy in copies_g:
            copy.start()
        first.wait()
        y_one, y_two, dy_one, dy_two = [held[i].astype(F32) for i in range(4)]

        def wait():
            for copy in copies_g:
                copy.wait()
            for copy in copies_f:
                copy.start()

    u = to_hdw(y_one)
    act, slope = silu_pair(u)
    act = act.astype(BF16).astype(F32)
    err = to_hdw(dy_two)
    ahead, back = convolve(act, err, wait, w_g, *bufs)
    x_two = (to_hdw(y_two) - ahead).astype(BF16).astype(F32)
    dx_one = (to_hdw(dy_one) + back * slope).astype(BF16).astype(F32)
    out[0] = to_dhw(x_two).astype(BF16)
    out[1] = to_dhw(dx_one).astype(BF16)
    act_two = silu_pair(x_two)[0]
    core, y, z = place[0], place[1], place[2]
    for b, a, e in ((F, act_two, dx_one), (G, act, err)):
        low, high = a[:, :HALF], a[:, HALF:]
        mine[b] = jnp.where(core == 0, low, high).astype(BF16)
        give[b, :VOX] = jnp.where(core == 0, high, low).astype(BF16)
        flipped = e.T.astype(BF16)
        for zz in range(NZ):
            for yy in range(NY):
                row = VOX + QUARTER * ((yy - y) & 3) + 16 * (zz ^ z)
                start = QUARTER * zz + 16 * yy
                give[b, pl.ds(pl.multiple_of(row, 16), 16)] = flipped[start : start + 16]
    if not picks:
        for copy in copies_f:
            copy.wait()


def half_f_kernel(place, *refs, picks):
    if picks:
        late, early, mid, feed, first_early, first_late, w_f, out, *bufs = refs
        chosen = feed.at[place[4]]
        y_one = pick(place, late[0].astype(F32), chosen[0].astype(F32))
        dy_two = pick(place, late[1].astype(F32), chosen[3].astype(F32))
    else:
        held, mid, w_f, out, *bufs = refs
        y_one, dy_two = held[0].astype(F32), held[3].astype(F32)
    x_two, dx_one = mid[0].astype(F32), mid[1].astype(F32)
    act, slope = silu_pair(to_hdw(x_two))
    act = act.astype(BF16).astype(F32)
    ahead, back = convolve(act, to_hdw(dx_one), lambda: None, w_f, *bufs)
    x_one = (y_one - to_dhw(ahead)).astype(BF16)
    dx_two = (dy_two + to_dhw(back * slope)).astype(BF16)
    if picks:
        out[0, 0] = first_late[0]
        out[0, 1] = first_early[0]
        out[0, 2] = first_early[1]
        out[0, 3] = first_late[1]
        out[1, 0] = x_one
        out[1, 1] = mid[0]
        out[1, 2] = mid[1]
        out[1, 3] = dx_two
    else:
        out[0] = x_one
        out[1] = dx_two


def call_half(kernel, place, args, out_shapes, picks, in_hbm=False):
    scratch = [pltpu.VMEM((VOX, 27 * CH), BF16)] * 2
    return pl.pallas_call(
        functools.partial(kernel, picks=picks),
        in_specs=[SMEM] + [HBM if in_hbm else VMEM] * len(args),
        out_specs=[VMEM] * len(out_shapes),
        scratch_shapes=scratch + ([pltpu.SemaphoreType.DMA((2 * CHUNKS + 1,))] if in_hbm else []),
        out_shape=[jax.ShapeDtypeStruct(s, BF16) for s in out_shapes],
        compiler_params=pltpu.CompilerParams(vmem_limit_bytes=20 << 20),
        cost_estimate=pl.CostEstimate(flops=4 * 27 * VOX * CH * CH, bytes_accessed=27 * CH * CH * 2, transcendentals=0),
    )(place, *args)


def pack_kernel(mine, give, got, *outs, groups):
    at = 0
    for branches in groups:
        for by in (1, 2, 3):
            out = outs[at]
            at += 1
            rows = slice(VOX + QUARTER * by, VOX + QUARTER * by + QUARTER)
            for i, b in enumerate(branches):
                out[i, 0, :VOX] = mine[b]
                out[i, 0, VOX:] = give[b, rows]
                out[i, 1, :VOX] = got[b, :VOX]
                out[i, 1, VOX:] = got[b, rows]


def gather_factors(give, mine, groups):
    got = dp_permute(give, lambda z, y, c: (z, y, c + 1))
    shapes = [
        jax.ShapeDtypeStruct((len(branches), 2, VOX + QUARTER, HALF), BF16) for branches in groups for _ in range(3)
    ]
    packed = pl.pallas_call(
        functools.partial(pack_kernel, groups=groups),
        out_shape=shapes,
        in_specs=[VMEM] * 3,
        out_specs=[VMEM] * len(shapes),
        compiler_params=pltpu.CompilerParams(vmem_limit_bytes=8 << 20),
        cost_estimate=pl.CostEstimate(flops=0, bytes_accessed=1 << 20, transcendentals=0),
    )(mine, give, got)
    parts = []
    for n in range(len(groups)):
        for by in (1, 2, 3):
            message = packed[3 * n + by - 1]
            parts.append(dp_permute(message, lambda z, y, c, by=by: (z, y + by, c)))
    return [(mine, give, got, *parts[3 * n : 3 * n + 3]) for n in range(len(groups))]


def products(refs, branch, at_part, lhs, rhs):
    mine, give, got, *parts = refs
    tiles = [(mine[branch], give[branch, VOX : VOX + QUARTER]), (got[branch, :VOX], got[branch, VOX : VOX + QUARTER])]
    for p in parts:
        for tile in range(2):
            tiles.append((p[at_part, tile, :VOX], p[at_part, tile, VOX:]))
    lane = lax.broadcasted_iota(jnp.int32, (QUARTER, VOX), 1)
    depth, width = (lane // TW) % TD, lane % TW
    zero = jnp.zeros((LINE, HALF), BF16)
    for index, (act, err) in enumerate(tiles):
        at = VOX * index
        rhs[0, at : at + LINE] = zero
        rhs[0, at + LINE : at + VOX] = act[: VOX - LINE]
        rhs[1, at : at + VOX] = act
        rhs[2, at : at + VOX - LINE] = act[LINE:]
        rhs[2, at + VOX - LINE : at + VOX] = zero
        err = err.astype(F32)
        for dd in (-1, 0, 1):
            for dw in (-1, 0, 1):
                x = err
                if dd or dw:
                    x = pltpu.roll(err, (TW * dd + dw) % VOX, 1)
                    ok = (depth - dd >= 0) & (depth - dd < TD) & (width - dw >= 0) & (width - dw < TW)
                    x = jnp.where(ok, x, 0.0)
                v = 3 * (dd + 1) + dw + 1
                lhs[QUARTER * v : QUARTER * v + QUARTER, at : at + VOX] = x.astype(BF16)
    return [jnp.dot(lhs[...], rhs[dh], preferred_element_type=F32) for dh in range(3)]


def first_grads_kernel(*refs):
    *ins, out, lhs, rhs = refs
    for branch in (F, G):
        for dh, value in enumerate(products(ins, branch, branch, lhs, rhs)):
            out[branch, dh] = value


def last_grads_kernel(*refs, branch):
    *ins, before, keep, send, lhs, rhs = refs
    for dh, value in enumerate(products(ins, branch, branch, lhs, rhs)):
        value = (value + before[branch, dh]).astype(BF16)
        for dd in range(3):
            for dw in range(3):
                for slots, out in ((KEEP[branch], keep), (SEND[branch], send)):
                    for i, slot in enumerate(slots):
                        row = QUARTER * (3 * dd + dw) + 16 * slot
                        out[i, 9 * dd + 3 * dh + dw] = value[row : row + 16]


def grad_call(kernel, ins, out_shape, flops):
    return pl.pallas_call(
        kernel,
        out_shape=out_shape,
        in_specs=[VMEM] * len(ins),
        out_specs=jax.tree.map(lambda s: VMEM, out_shape),
        scratch_shapes=[pltpu.VMEM((9 * QUARTER, 8 * VOX), BF16), pltpu.VMEM((3, 8 * VOX, HALF), BF16)],
        compiler_params=pltpu.CompilerParams(vmem_limit_bytes=24 << 20),
        cost_estimate=pl.CostEstimate(flops=flops, bytes_accessed=4 << 20, transcendentals=0),
    )(*ins)


def small_call(kernel, ins, out_shape):
    return pl.pallas_call(
        kernel,
        out_shape=out_shape,
        in_specs=ins[0],
        out_specs=jax.tree.map(lambda s: VMEM, out_shape),
        compiler_params=pltpu.CompilerParams(vmem_limit_bytes=8 << 20),
        cost_estimate=pl.CostEstimate(flops=0, bytes_accessed=1 << 20, transcendentals=0),
    )(*ins[1])


def middle_kernel(keep, got, own, other):
    own[...] = keep[0].astype(F32) + got[0].astype(F32)
    other[...] = (keep[1].astype(F32) + got[1].astype(F32)).astype(BF16)


def reduce_z(keep, send, branch):
    got = dp_permute(send, lambda z, y, c: (z ^ FIRST[branch], y, c))
    piece = (27, 16, HALF)
    own, other = small_call(
        middle_kernel, ([VMEM] * 2, (keep, got)), [jax.ShapeDtypeStruct(piece, F32), jax.ShapeDtypeStruct(piece, BF16)]
    )
    return own, dp_permute(other, lambda z, y, c: (z ^ SECOND[branch], y, c))


def total_kernel(place, own_f, last_f, own_g, last_g, mine, give):
    first = place[0] == 0
    for branch, own, last in ((F, own_f, last_f), (G, own_g, last_g)):
        total = own[...] + last[...].astype(F32)
        low, high = total[:, :8], total[:, 8:]
        mine[branch] = jnp.where(first, low, high)
        give[branch] = jnp.where(first, high, low).astype(BF16)


def update_kernel(place, mine, got, momentum, out, *, scale):
    first = place[0] == 0
    for branch in (F, G):
        own, other = mine[branch], got[branch].astype(F32)
        low = jnp.where(first, own, other)
        high = jnp.where(first, other, own)
        out[branch, :, :, :HALF] = 0.9 * momentum[branch, :, :, :HALF] + low * scale
        out[branch, :, :, HALF:] = 0.9 * momentum[branch, :, :, HALF:] + high * scale


def steps(incoming, feed, plan, weights, momentum):
    replicas = lax.axis_size("dp")
    rank = lax.axis_index("dp")
    z, y, c = rank // (NY * NC), (rank // NC) % NY, rank % NC
    is_last = (lax.axis_index("section") == lax.axis_size("section") - 1).astype(jnp.int32)
    slot = jnp.arange(8, dtype=jnp.int32)
    place = jnp.zeros((8,), jnp.int32)
    for i, value in enumerate((c, y, z, is_last, plan[0, 0])):
        place = jnp.where(slot == i, value, place)
    weights = pltpu.with_memory_space_constraint(weights[0], pltpu.HBM)
    incoming = pltpu.with_memory_space_constraint(incoming[0], pltpu.HBM)
    pair = (2, VOX, CH)
    mid_shapes = [pair, (2, VOX + CH, HALF), (2, VOX, HALF)]
    early, give, mine, held, w_g, w_f = call_half(
        half_g_kernel,
        place,
        [incoming, weights],
        [*mid_shapes, (4, VOX, CH), (27, CH, CH), (27, CH, CH)],
        False,
        in_hbm=True,
    )
    (factors0,) = gather_factors(give, mine, ((F, G),))
    (late,) = call_half(half_f_kernel, place, [held, early, w_f], [pair], False)
    y_early, y_late = from_next_section(early), from_next_section(late)
    flops = 4 * 27 * QUARTER * HALF * 8 * VOX
    before = grad_call(first_grads_kernel, factors0, jax.ShapeDtypeStruct((2, 3, 9 * QUARTER, HALF), F32), flops)
    mid, give, mine = call_half(half_g_kernel, place, [y_late, y_early, feed, w_g], mid_shapes, True)
    (factors1,) = gather_factors(give, mine, ((F, G),))
    (upstream,) = call_half(
        half_f_kernel, place, [y_late, y_early, mid, feed, early, late, w_f], [(2, 4, VOX, CH)], True
    )
    terms = {}
    block = jax.ShapeDtypeStruct((2, 27, 16, HALF), BF16)
    for branch in (G, F):
        keep, send = grad_call(
            functools.partial(last_grads_kernel, branch=branch), (*factors1, before), [block, block], flops // 2
        )
        terms[branch] = reduce_z(keep, send, branch)
    piece = (2, 27, 8, HALF)
    mine, give = small_call(
        total_kernel,
        ([SMEM] + [VMEM] * 4, (place, *terms[F], *terms[G])),
        [jax.ShapeDtypeStruct(piece, F32), jax.ShapeDtypeStruct(piece, BF16)],
    )
    got = dp_permute(give, lambda z, y, c: (z, y, 1 - c))
    new = small_call(
        functools.partial(update_kernel, scale=1.0 / (replicas * TICKS)),
        ([SMEM] + [VMEM] * 3, (place, mine, got, momentum[0])),
        jax.ShapeDtypeStruct(momentum.shape[1:], F32),
    )
    return (upstream[:, None], new[None])


def solution(mesh):
    in_specs = (
        P("section", None, "dp", None),
        P(None, None, "dp", None),
        P(None, "dp"),
        P("section", None, None, None, None),
        P("section", None, None, "dp", None),
    )
    out_specs = (P(None, "section", None, "dp", None), P("section", None, None, "dp", None))
    return jax.shard_map(steps, mesh=mesh, in_specs=in_specs, out_specs=out_specs, check_vma=False)
```

```python
import functools

import jax
import jax.numpy as jnp
from jax import lax
from jax.experimental import pallas as pl
from jax.experimental.pallas import tpu as pltpu
from jax.sharding import PartitionSpec as P


TD, TH, TW = 2, 8, 8
VOX = TD * TH * TW
CH = 256
HALF = 128
LINE = TD * TW
TICKS = 2
NZ, NY, NC = 4, 4, 2
QUARTER = 64
F32, BF16 = jnp.float32, jnp.bfloat16
F, G = 0, 1
FIRST = (1, 3)
SECOND = (3, 1)
CHUNKS = 3
PIECE = (27, 8, CH)
VMEM = pl.BlockSpec(memory_space=pltpu.VMEM)
SMEM = pl.BlockSpec(memory_space=pltpu.SMEM)
HBM = pl.BlockSpec(memory_space=pltpu.HBM)


def rank_of(z, y, c):
    return ((z % NZ) * NY + y % NY) * NC + c % NC


def dp_permute(array, move):
    pairs = []
    for z in range(NZ):
        for y in range(NY):
            for c in range(NC):
                pairs.append((rank_of(z, y, c), rank_of(*move(z, y, c))))
    return lax.ppermute(array, "dp", pairs)


def from_next_section(array):
    size = lax.axis_size("section")
    return lax.ppermute(array, "section", [(i, i - 1) for i in range(1, size)])


def to_hdw(x):
    return jnp.concatenate([x[64 * d + 8 * h : 64 * d + 8 * h + 8] for h in range(TH) for d in range(TD)], axis=0)


def to_dhw(x):
    return jnp.concatenate([x[16 * h + 8 * d : 16 * h + 8 * d + 8] for d in range(TD) for h in range(TH)], axis=0)


def silu_pair(u):
    sig = jax.nn.sigmoid(u)
    return u * sig, sig * (1.0 + u * (1.0 - sig))


def moved(x, dd, dw):
    row = lax.broadcasted_iota(jnp.int32, x.shape, 0)
    ok = None
    if dw:
        x = pltpu.roll(x, (-dw) % VOX, 0)
        w = row % TW + dw
        ok = (w >= 0) & (w < TW)
    if dd:
        pieces = [x[LINE * h + 8 * (1 - d) : LINE * h + 8 * (1 - d) + 8] for h in range(TH) for d in range(TD)]
        x = jnp.concatenate(pieces, axis=0)
        d = (row // TW) % TD + dd
        inside = (d >= 0) & (d < TD)
        ok = inside if ok is None else ok & inside
    if ok is not None:
        x = jnp.where(ok, x, 0.0)
    return x.astype(BF16)


def fill(buf, x, sign):
    zero = jnp.zeros((LINE, CH), BF16)
    for dd in (-1, 0, 1):
        for dw in (-1, 0, 1):
            m = moved(x, sign * dd, sign * dw)
            for dh in (-1, 0, 1):
                t = 9 * (dd + 1) + 3 * (dh + 1) + dw + 1
                cols = slice(CH * t, CH * t + CH)
                if sign * dh == 0:
                    buf[:, cols] = m
                elif sign * dh == 1:
                    buf[: VOX - LINE, cols] = m[LINE:]
                    buf[VOX - LINE :, cols] = zero
                else:
                    buf[LINE:, cols] = m[: VOX - LINE]
                    buf[:LINE, cols] = zero


def convolve(act, err, wait, w_ref, buf_a, buf_e):
    fill(buf_a, act, 1)
    fill(buf_e, err, -1)
    wait()
    back = jnp.dot(buf_e[...], w_ref[...].reshape(27 * CH, CH), preferred_element_type=F32)
    ahead = None
    for t in range(27):
        term = lax.dot_general(
            buf_a[:, CH * t : CH * t + CH], w_ref[t], (((1,), (1,)), ((), ())), preferred_element_type=F32
        )
        ahead = term if ahead is None else ahead + term
    return ahead, back


def pick(place, below, chosen):
    return jnp.where(place[3] == 1, chosen, below)


def fetches(w_hbm, w_vmem, branch, sems):
    size = 27 // CHUNKS
    copies = []
    for k in range(CHUNKS):
        taps = pl.ds(size * k, size)
        copies.append(pltpu.make_async_copy(w_hbm.at[branch, taps], w_vmem.at[taps], sems.at[CHUNKS * branch + k]))
    return copies


def half_g_kernel(place, *refs, picks):
    if picks:
        below, feed, w_g, out, give, mine, *bufs = refs
        chosen = feed.at[place[4]]
        y_one, y_two, dy_one, dy_two = [pick(place, below[i].astype(F32), chosen[i].astype(F32)) for i in range(4)]

        def wait():
            pass

    else:
        incoming, w_hbm, out, give, mine, held, w_g, w_f, *bufs, sems = refs
        first = pltpu.make_async_copy(incoming, held, sems.at[2 * CHUNKS])
        first.start()
        copies_g, copies_f = fetches(w_hbm, w_g, G, sems), fetches(w_hbm, w_f, F, sems)
        for copy in copies_g:
            copy.start()
        first.wait()
        y_one, y_two, dy_one, dy_two = [held[i].astype(F32) for i in range(4)]

        def wait():
            for copy in copies_f:
                copy.start()
            for copy in copies_g:
                copy.wait()

    u = to_hdw(y_one)
    act, slope = silu_pair(u)
    act = act.astype(BF16).astype(F32)
    err = to_hdw(dy_two)
    ahead, back = convolve(act, err, wait, w_g, *bufs)
    x_two = (to_hdw(y_two) - ahead).astype(BF16).astype(F32)
    dx_one = (to_hdw(dy_one) + back * slope).astype(BF16).astype(F32)
    out[0] = to_dhw(x_two).astype(BF16)
    out[1] = to_dhw(dx_one).astype(BF16)
    act_two = silu_pair(x_two)[0]
    first, y, z = place[0] == 0, place[1], place[2]
    for part, over_z, a, e in (
        (mine, first, jnp.where(first, act, act_two), jnp.where(first, err, dx_one)),
        (give, jnp.logical_not(first), jnp.where(first, act_two, act), jnp.where(first, dx_one, err)),
    ):
        part[:VOX] = a[:, :HALF].astype(BF16)
        part[VOX : 2 * VOX] = a[:, HALF:].astype(BF16)
        flipped = e.T.astype(BF16)
        for zz in range(NZ):
            for yy in range(NY):
                row = jnp.where(
                    over_z, QUARTER * ((zz - z) & 3) + 16 * (yy ^ y), QUARTER * ((yy - y) & 3) + 16 * (zz ^ z)
                )
                row = 2 * VOX + row
                start = QUARTER * zz + 16 * yy
                part[pl.ds(pl.multiple_of(row, 16), 16)] = flipped[start : start + 16]
    if not picks:
        for copy in copies_f:
            copy.wait()


def half_f_kernel(place, *refs, picks):
    if picks:
        below, mid, feed, first_out, w_f, out, *bufs = refs
        chosen = feed.at[place[4]]
        y_one = pick(place, below[0].astype(F32), chosen[0].astype(F32))
        dy_two = pick(place, below[3].astype(F32), chosen[3].astype(F32))
        out[0] = first_out[...]
        out = out.at[1]
    else:
        held, mid, w_f, out, *bufs = refs
        y_one, dy_two = held[0].astype(F32), held[3].astype(F32)
    x_two, dx_one = mid[0].astype(F32), mid[1].astype(F32)
    act, slope = silu_pair(to_hdw(x_two))
    act = act.astype(BF16).astype(F32)
    ahead, back = convolve(act, to_hdw(dx_one), lambda: None, w_f, *bufs)
    x_one = (y_one - to_dhw(ahead)).astype(BF16)
    dx_two = (dy_two + to_dhw(back * slope)).astype(BF16)
    out[0] = x_one
    out[1] = mid[0]
    out[2] = mid[1]
    out[3] = dx_two


def call_half(kernel, place, args, out_shapes, picks, in_hbm=False):
    scratch = [pltpu.VMEM((VOX, 27 * CH), BF16)] * 2
    return pl.pallas_call(
        functools.partial(kernel, picks=picks),
        in_specs=[SMEM] + [HBM if in_hbm else VMEM] * len(args),
        out_specs=[VMEM] * len(out_shapes),
        scratch_shapes=scratch + ([pltpu.SemaphoreType.DMA((2 * CHUNKS + 1,))] if in_hbm else []),
        out_shape=[jax.ShapeDtypeStruct(s, BF16) for s in out_shapes],
        compiler_params=pltpu.CompilerParams(vmem_limit_bytes=20 << 20),
        cost_estimate=pl.CostEstimate(flops=4 * 27 * VOX * CH * CH, bytes_accessed=27 * CH * CH * 2, transcendentals=0),
    )(place, *args)


def small_call(kernel, ins, out_shape):
    return pl.pallas_call(
        kernel,
        out_shape=out_shape,
        in_specs=ins[0],
        out_specs=jax.tree.map(lambda s: VMEM, out_shape),
        compiler_params=pltpu.CompilerParams(vmem_limit_bytes=8 << 20),
        cost_estimate=pl.CostEstimate(flops=0, bytes_accessed=1 << 20, transcendentals=0),
    )(*ins[1])


def pack_kernel(mine, got, *outs):
    for by, out in zip((1, 2, 3), outs):
        rows = slice(2 * VOX + QUARTER * by, 2 * VOX + QUARTER * by + QUARTER)
        for tile, part in enumerate((mine, got)):
            out[tile, : 2 * VOX] = part[: 2 * VOX]
            out[tile, 2 * VOX :] = part[rows]


def gather_factors(give, mine):
    got = dp_permute(give, lambda z, y, c: (z, y, 1 - c))
    shape = jax.ShapeDtypeStruct((2, 2 * VOX + QUARTER, HALF), BF16)
    packed = small_call(pack_kernel, ([VMEM] * 2, (mine, got)), [shape] * 3)
    parts = [
        dp_permute(message, lambda z, y, c, by=by: (z, y + by, c) if c else (z + by, y, c))
        for by, message in zip((1, 2, 3), packed)
    ]
    return mine, got, *parts


def products(refs, lhs, rhs):
    mine, got, *parts = refs
    tiles = []
    for part in (mine, got, *(p.at[tile] for p in parts for tile in range(2))):
        act = jnp.concatenate([part[:VOX], part[VOX : 2 * VOX]], axis=1)
        tiles.append((act, part[2 * VOX : 2 * VOX + QUARTER]))
    lane = lax.broadcasted_iota(jnp.int32, (QUARTER, VOX), 1)
    depth, width = (lane // TW) % TD, lane % TW
    zero = jnp.zeros((LINE, CH), BF16)
    for index, (act, err) in enumerate(tiles):
        at = VOX * index
        rhs[0, at : at + LINE] = zero
        rhs[0, at + LINE : at + VOX] = act[: VOX - LINE]
        rhs[1, at : at + VOX] = act
        rhs[2, at : at + VOX - LINE] = act[LINE:]
        rhs[2, at + VOX - LINE : at + VOX] = zero
        err = err.astype(F32)
        for dd in (-1, 0, 1):
            for dw in (-1, 0, 1):
                x = err
                if dd or dw:
                    x = pltpu.roll(err, (TW * dd + dw) % VOX, 1)
                    ok = (depth - dd >= 0) & (depth - dd < TD) & (width - dw >= 0) & (width - dw < TW)
                    x = jnp.where(ok, x, 0.0)
                v = 3 * (dd + 1) + dw + 1
                lhs[QUARTER * v : QUARTER * v + QUARTER, at : at + VOX] = x.astype(BF16)
    return [jnp.dot(lhs[...], rhs[dh], preferred_element_type=F32) for dh in range(3)]


def first_grads_kernel(*refs):
    *ins, out, lhs, rhs = refs
    for dh, value in enumerate(products(ins, lhs, rhs)):
        out[dh] = value


def last_grads_kernel(*refs):
    *ins, before, keep, send_0, send_1, lhs, rhs = refs
    for dh, value in enumerate(products(ins, lhs, rhs)):
        value = value + before[dh]
        for dd in range(3):
            for dw in range(3):
                tap = 9 * dd + 3 * dh + dw
                for core, send in ((0, send_0), (1, send_1)):
                    row = QUARTER * (3 * dd + dw) + 8 * core
                    rows = [slice(row + 16 * slot, row + 16 * slot + 8) for slot in (0, SECOND[core], FIRST[core], 2)]
                    keep[core, 0, tap] = value[rows[0]].astype(BF16)
                    keep[core, 1, tap] = value[rows[1]].astype(BF16)
                    send[0, tap] = value[rows[2]].astype(BF16)
                    send[1, tap] = value[rows[3]].astype(BF16)


def grad_call(kernel, ins, out_shape, flops):
    return pl.pallas_call(
        kernel,
        out_shape=out_shape,
        in_specs=[VMEM] * len(ins),
        out_specs=jax.tree.map(lambda s: VMEM, out_shape),
        scratch_shapes=[pltpu.VMEM((9 * QUARTER, 8 * VOX), BF16), pltpu.VMEM((3, 8 * VOX, CH), BF16)],
        compiler_params=pltpu.CompilerParams(vmem_limit_bytes=24 << 20),
        cost_estimate=pl.CostEstimate(flops=flops, bytes_accessed=4 << 20, transcendentals=0),
    )(*ins)


def middle_kernel(place, keep, got_0, got_1, mine, same, cross, swap):
    first = place[0] == 0
    own, other = [], []
    for core, got in ((0, got_0), (1, got_1)):
        own.append(keep[core, 0].astype(F32) + got[0].astype(F32))
        other.append(keep[core, 1].astype(F32) + got[1].astype(F32))
    mine[...] = jnp.where(first, own[0], own[1])
    swap[...] = jnp.where(first, own[1], own[0]).astype(BF16)
    same[...] = jnp.where(first, other[0], other[1]).astype(BF16)
    cross[...] = jnp.where(first, other[1], other[0]).astype(BF16)


def reduced(z, y, c, by, to):
    return (z ^ by, y, to) if c else (z, y ^ by, to)


def reduce_all(place, keep, sends):
    got = [dp_permute(send, lambda z, y, c, by=FIRST[core]: reduced(z, y, c, by, c)) for core, send in enumerate(sends)]
    mine, same, cross, swap = small_call(
        middle_kernel,
        ([SMEM] + [VMEM] * 3, (place, keep, *got)),
        [jax.ShapeDtypeStruct(PIECE, F32)] + [jax.ShapeDtypeStruct(PIECE, BF16)] * 3,
    )
    same = dp_permute(same, lambda z, y, c: reduced(z, y, c, SECOND[c], c))
    cross = dp_permute(cross, lambda z, y, c: reduced(z, y, c, SECOND[1 - c], 1 - c))
    swap = dp_permute(swap, lambda z, y, c: (z, y, 1 - c))
    return mine, same, cross, swap


def update_kernel(place, mine, same, cross, swap, momentum, out, *, scale):
    first = place[0] == 0
    own = mine[...] + same[...].astype(F32)
    other = cross[...].astype(F32) + swap[...].astype(F32)
    out[F] = 0.9 * momentum[F] + jnp.where(first, other, own) * scale
    out[G] = 0.9 * momentum[G] + jnp.where(first, own, other) * scale


def steps(incoming, feed, plan, weights, momentum):
    replicas = lax.axis_size("dp")
    rank = lax.axis_index("dp")
    z, y, c = rank // (NY * NC), (rank // NC) % NY, rank % NC
    is_last = (lax.axis_index("section") == lax.axis_size("section") - 1).astype(jnp.int32)
    slot = jnp.arange(8, dtype=jnp.int32)
    place = jnp.zeros((8,), jnp.int32)
    for i, value in enumerate((c, y, z, is_last, plan[0, 0])):
        place = jnp.where(slot == i, value, place)
    weights = pltpu.with_memory_space_constraint(weights[0], pltpu.HBM)
    incoming = pltpu.with_memory_space_constraint(incoming[0], pltpu.HBM)
    pair = (2, VOX, CH)
    mid_shapes = [pair, (2 * VOX + CH, HALF), (2 * VOX + CH, HALF)]
    early, give, mine, held, w_g, w_f = call_half(
        half_g_kernel,
        place,
        [incoming, weights],
        [*mid_shapes, (4, VOX, CH), (27, CH, CH), (27, CH, CH)],
        False,
        in_hbm=True,
    )
    factors0 = gather_factors(give, mine)
    (first_out,) = call_half(half_f_kernel, place, [held, early, w_f], [(4, VOX, CH)], False)
    below = from_next_section(first_out)
    flops = 4 * 27 * QUARTER * HALF * 8 * VOX
    before = grad_call(first_grads_kernel, factors0, jax.ShapeDtypeStruct((3, 9 * QUARTER, CH), F32), flops)
    mid, give, mine = call_half(half_g_kernel, place, [below, feed, w_g], mid_shapes, True)
    factors1 = gather_factors(give, mine)
    (upstream,) = call_half(half_f_kernel, place, [below, mid, feed, first_out, w_f], [(2, 4, VOX, CH)], True)
    block = jax.ShapeDtypeStruct((2, *PIECE), BF16)
    keep, *sends = grad_call(
        last_grads_kernel, (*factors1, before), [jax.ShapeDtypeStruct((2, 2, *PIECE), BF16), block, block], flops
    )
    new = small_call(
        functools.partial(update_kernel, scale=1.0 / (replicas * TICKS)),
        ([SMEM] + [VMEM] * 5, (place, *reduce_all(place, keep, sends), momentum[0])),
        jax.ShapeDtypeStruct(momentum.shape[1:], F32),
    )
    return (upstream[:, None], new[None])


def solution(mesh):
    in_specs = (
        P("section", None, "dp", None),
        P(None, None, "dp", None),
        P(None, "dp"),
        P("section", None, None, None, None),
        P("section", None, None, "dp", None),
    )
    out_specs = (P(None, "section", None, "dp", None), P("section", None, None, "dp", None))
    return jax.shard_map(steps, mesh=mesh, in_specs=in_specs, out_specs=out_specs, check_vma=False)
```
